256 devices in a mesh: dp: 4 (over y), sy: 4 (over z_lo, core), sx: 16 (over x, z_hi).
Axes of the slice: x: 4, y: 4, z: 8 (z_hi: 4, z_lo: 2; z = z_hi * 2 + z_lo), core: 2. Of those that a mesh axis runs over, the one named last changes fastest.
Arguments:
- inputs: bfloat16 [4, 8, 32, 32, 512], P('dp', None, 'sy', 'sx'), may hold values from -6 to 6
- pre_activation: bfloat16 [4, 8, 32, 32, 512], P('dp', None, 'sy', 'sx'), may hold values from -6 to 6
- upstream: bfloat16 [4, 8, 32, 32, 512], P('dp', None, 'sy', 'sx'), may hold values from -6 to 6
- weight: bfloat16 [27, 512, 512], P(None, 'dp'), may hold values from -0.0546875 to 0.0546875
- first_moment: float32 [13824, 128], P(('dp', 'sy', 'sx')), may hold values from -4 to 4
- second_moment: float32 [13824, 128], P(('dp', 'sy', 'sx')), may hold values from 0.05 to 1
- hash_seed: int32 [], replicated, may hold values from 0 to 999999
- step_count: int32 [], replicated, may hold values from 1 to 29
Outputs:
- input_grad: bfloat16 [4, 8, 32, 32, 512], P('dp', None, 'sy', 'sx')
- new_first: float32 [13824, 128], P(('dp', 'sy', 'sx'))
- new_second: float32 [13824, 128], P(('dp', 'sy', 'sx'))
- scales: float32 [13824], P(('dp', 'sy', 'sx'))
The draws below stay inside these ranges and needn't reach their ends.
All inputs are finite; a program needn't handle non-finite values.
Results may differ from the reference program's by a relative error of at most 0.004.
Values may be sent and summed in bfloat16 or wider, within the bound.
No kernel may reach another device: no remote copies, remote signals or barrier semaphores. Data moves between devices by JAX's collectives and lax.ppermute only.
A program may use at most 128 MiB of HBM per device.

```python
import math
import jax
import jax.numpy as jnp
from jax import lax

IN_CHANNELS = 512
OUT_CHANNELS = 512
LOW_RANK = 128
FRAMES = 8
SAMPLES = 4
HEIGHT = 32
WIDTH = 32
TOKENS = 32768
GRAD_ROWS = 13824


def raised(result, rng, source, target, blocks, factor):
    owner, partner = [(jnp.arange(result.shape[position]) // (result.shape[position] // blocks)).reshape([-1 if axis == position else 1 for axis in range(result.ndim)]) for position in (source, target)]
    chosen = jax.random.permutation(rng, blocks)[partner]
    strong = (owner == chosen) | (owner == (partner + blocks // 2) % blocks)
    return jnp.where(strong, factor * result, result)


def block_scale(rng, dims, shards, smallest, high):
    loudness, own = 1.0, jax.random.fold_in(rng, 6)
    for position, parts in shards:
        draws = jnp.exp(jax.random.uniform(jax.random.fold_in(own, position), (parts,), jnp.float32, smallest / len(shards), high / len(shards)))
        loudness = loudness * jnp.repeat(draws, dims[position] // parts).reshape([-1 if axis == position else 1 for axis in range(len(dims))])
    return loudness


def bell_draw(own_key, extent, width, reach, split=(), held_as=jnp.bfloat16):
    result = jax.random.normal(own_key, extent, jnp.float32) * width
    if len(split) > 0:
        result = block_scale(own_key, extent, split, -0.22, 0.18) * result
    return jnp.clip(result, min=-reach, max=reach).astype(held_as)


def bell_draw_with(key, dims, deviation, bound, cuts, heavy, held_as=jnp.bfloat16):
    entries = deviation * jax.random.normal(key, dims, jnp.float32)
    if cuts:
        entries = entries * block_scale(key, dims, cuts, -0.22, 0.18)
    return jnp.clip(raised(entries, jax.random.fold_in(key, 3), *heavy), -bound, bound).astype(held_as)


def setup_inputs(seed: int = 0) -> dict:
    seeds = jax.random.split(jax.random.key(seed), 9)
    return {
        "inputs": bell_draw_with(seeds[0], (SAMPLES, FRAMES, HEIGHT, WIDTH, IN_CHANNELS), 1.0, 6.0, ((0, 4), (2, 4), (3, 16)), (3, 4, 16, 2.0)),
        "pre_activation": bell_draw(seeds[1], (SAMPLES, FRAMES, HEIGHT, WIDTH, OUT_CHANNELS), 1.5, 6.0, ((0, 4), (2, 4), (3, 16))),
        "upstream": bell_draw(seeds[2], (SAMPLES, FRAMES, HEIGHT, WIDTH, OUT_CHANNELS), 1.0, 6.0, ((0, 4), (2, 4), (3, 16))),
        "weight": bell_draw(seeds[3], (27, IN_CHANNELS, OUT_CHANNELS), (27 * IN_CHANNELS) ** -0.5, 0.0546875, ((1, 4),)),
        "first_moment": bell_draw(seeds[4], (GRAD_ROWS, LOW_RANK), 0.5, 4.0, ((0, 256),), jnp.float32),
        "second_moment": jnp.clip(jnp.exp(math.log(1.0) - 2.9957323 * jax.random.uniform(seeds[5], (GRAD_ROWS, LOW_RANK), jnp.float32) ** block_scale(seeds[5], (GRAD_ROWS, LOW_RANK), ((0, 256),), -0.2, 0.2)), 0.05, 1.0),
        "hash_seed": jax.random.randint(seeds[6], (), 0, 1000000).astype(jnp.int32),
        "step_count": jax.random.randint(seeds[7], (), 1, 30).astype(jnp.int32),
    }


def projection(hash_seed, rows_count, cols_count):
    row_ids = lax.broadcasted_iota(jnp.int32, (rows_count, cols_count), 0)
    col_ids = lax.broadcasted_iota(jnp.int32, (rows_count, cols_count), 1)
    mixed = (row_ids * cols_count + col_ids) * jnp.int32(-1640531535) + hash_seed * jnp.int32(668265263)
    mixed = mixed ^ lax.shift_right_logical(mixed, jnp.int32(15))
    mixed = mixed * jnp.int32(-2048144777)
    mixed = mixed ^ lax.shift_right_logical(mixed, jnp.int32(13))
    mixed = mixed * jnp.int32(-1028477379)
    mixed = mixed ^ lax.shift_right_logical(mixed, jnp.int32(16))
    level = (lax.shift_right_logical(mixed, jnp.int32(8)) & jnp.int32(65535)).astype(jnp.float32)
    return ((level + 0.5) * (2.0 / 65536.0) - 1.0) * math.sqrt(3.0 / cols_count)

def reference(inputs, pre_activation, upstream, weight, first_moment, second_moment, hash_seed, step_count):
    pre_value = pre_activation.astype(jnp.float32)
    upstream_value = upstream.astype(jnp.float32)
    sigmoid_value = jax.nn.sigmoid(pre_value)
    grad_pre = (upstream_value * sigmoid_value * (1.0 + pre_value * (1.0 - sigmoid_value))).astype(jnp.bfloat16)
    projector = projection(hash_seed, OUT_CHANNELS, LOW_RANK).astype(jnp.bfloat16)
    proj_grad = jnp.dot(grad_pre.reshape(TOKENS, OUT_CHANNELS), projector, preferred_element_type=jnp.float32)
    proj_grad = proj_grad.astype(jnp.bfloat16).reshape(SAMPLES, FRAMES, HEIGHT, WIDTH, LOW_RANK)
    pad_spec = ((0, 0), (1, 1), (1, 1), (1, 1), (0, 0))
    grad_padded = jnp.pad(grad_pre, pad_spec)
    proj_padded = jnp.pad(proj_grad, pad_spec)
    flat_source = inputs.reshape(TOKENS, IN_CHANNELS)
    branch = jnp.zeros((TOKENS, IN_CHANNELS), jnp.float32)
    terms = []
    for offset in range(27):
        along_t = 2 - offset // 9
        along_h = 2 - offset // 3 % 3
        along_w = 2 - offset % 3
        shifted = grad_padded[:, along_t:along_t + FRAMES, along_h:along_h + HEIGHT, along_w:along_w + WIDTH, :]
        branch = branch + jnp.dot(shifted.reshape(TOKENS, OUT_CHANNELS), weight[offset].T, preferred_element_type=jnp.float32)
        shifted_proj = proj_padded[:, along_t:along_t + FRAMES, along_h:along_h + HEIGHT, along_w:along_w + WIDTH, :]
        terms.append(jnp.dot(flat_source.T, shifted_proj.reshape(TOKENS, LOW_RANK), preferred_element_type=jnp.float32))
    input_grad = (upstream_value.reshape(TOKENS, IN_CHANNELS) + branch).astype(jnp.bfloat16)
    input_grad = input_grad.reshape(SAMPLES, FRAMES, HEIGHT, WIDTH, IN_CHANNELS)
    reduced = jnp.stack(terms, axis=1).reshape(IN_CHANNELS * 27, LOW_RANK) / math.sqrt(TOKENS)
    new_first = 0.9 * first_moment + 0.1 * reduced
    new_second = 0.999 * second_moment + 0.001 * reduced * reduced
    step_value = step_count.astype(jnp.float32)
    first_bias = 1.0 - jnp.power(jnp.float32(0.9), step_value)
    second_bias = 1.0 - jnp.power(jnp.float32(0.999), step_value)
    adapted = new_first / first_bias / (jnp.sqrt(new_second / second_bias) + 1e-08)
    scales = jnp.sqrt(lax.optimization_barrier(jnp.mean(adapted * adapted, axis=1))) / jnp.sqrt(lax.optimization_barrier(jnp.mean(reduced * reduced, axis=1)) + 1e-06)
    return (input_grad, new_first, new_second, scales)
```

```python
import math

import jax
import jax.numpy as jnp
from jax import lax
from jax.experimental import pallas as pl
from jax.experimental.pallas import tpu as pltpu
from jax.sharding import Mesh, PartitionSpec as P

BF16 = jnp.bfloat16
F32 = jnp.float32


def _call(body, outs, scratch=(), smem=0, total=0):
    specs = [pl.BlockSpec(memory_space=pltpu.SMEM)] * smem
    specs += [pl.BlockSpec(memory_space=pltpu.VMEM)] * (total - smem)
    return pl.pallas_call(
        body,
        out_shape=outs,
        in_specs=specs,
        out_specs=jax.tree.map(lambda _: pl.BlockSpec(memory_space=pltpu.VMEM), outs),
        scratch_shapes=list(scratch),
        compiler_params=pltpu.CompilerParams(vmem_limit_bytes=40 * 1024 * 1024),
        name=body.__name__,
    )


def _rows_to_scratch(ref, scratch):
    frames, rows, cols, _ = ref.shape
    for t in range(frames):
        for h in range(rows):
            base = (t * rows + h) * cols
            row = ref[t, h].astype(F32)
            for tile in range(scratch.shape[0]):
                scratch[tile, base : base + cols, :] = row[:, tile * 128 : tile * 128 + 128]


def _token_major(scratch, frames, rows, cols):
    tiles = []
    for tile in range(scratch.shape[0]):
        tiles.append(
            jnp.concatenate(
                [
                    scratch[tile, pl.ds(h * cols + w, frames, stride=rows * cols), :]
                    for w in range(cols)
                    for h in range(rows)
                ],
                axis=0,
            )
        )
    return jnp.concatenate(tiles, axis=1)


def prepare(seed, pre, up, inp, g_out, proj_out, in_out, top_out, bot_out, s_pre, s_up, s_in):
    frames, rows, cols, chans = pre.shape
    rank = proj_out.shape[-1]
    _rows_to_scratch(pre, s_pre)
    _rows_to_scratch(up, s_up)
    _rows_to_scratch(inp, s_in)

    row_ids = lax.broadcasted_iota(jnp.int32, (chans, rank), 0)
    col_ids = lax.broadcasted_iota(jnp.int32, (chans, rank), 1)
    mixed = (row_ids * rank + col_ids) * jnp.int32(-1640531535) + seed[0] * jnp.int32(668265263)
    mixed = mixed ^ lax.shift_right_logical(mixed, jnp.int32(15))
    mixed = mixed * jnp.int32(-2048144777)
    mixed = mixed ^ lax.shift_right_logical(mixed, jnp.int32(13))
    mixed = mixed * jnp.int32(-1028477379)
    mixed = mixed ^ lax.shift_right_logical(mixed, jnp.int32(16))
    level = (lax.shift_right_logical(mixed, jnp.int32(8)) & jnp.int32(65535)).astype(F32)
    projector = (((level + 0.5) * (2.0 / 65536.0) - 1.0) * math.sqrt(3.0 / rank)).astype(BF16)

    x = _token_major(s_pre, frames, rows, cols)
    u = _token_major(s_up, frames, rows, cols)
    sig = jax.nn.sigmoid(x)
    g = (u * sig * (1.0 + x * (1.0 - sig))).astype(BF16)
    proj = jnp.dot(g, projector, preferred_element_type=F32).astype(BF16)
    g4 = g.reshape(cols, rows, frames, chans)
    p4 = proj.reshape(cols, rows, frames, rank)
    g_out[...] = g4
    proj_out[...] = p4
    top_out[:, :, :chans] = g4[:, 0]
    bot_out[:, :, :chans] = g4[:, rows - 1]
    top_out[:, :, chans:] = p4[:, 0]
    bot_out[:, :, chans:] = p4[:, rows - 1]

    dest = in_out.shape[0]
    r = lax.broadcasted_iota(jnp.int32, (chans, chans), 0)
    c = lax.broadcasted_iota(jnp.int32, (chans, chans), 1)
    target = (r & 1) * 16 + ((r >> 1) & 15) * 32 + (r >> 5)
    perm = jnp.where(c == target, 1.0, 0.0).astype(BF16)
    moved = jnp.dot(
        _token_major(s_in, frames, rows, cols).astype(BF16), perm, preferred_element_type=F32
    ).reshape(cols, 4, rows // 4, frames, chans)
    lanes = lax.broadcasted_iota(jnp.int32, (cols * (rows // 4) * frames, 128), 1)
    for tile in range(dest // 4):
        groups = [
            moved[:, q, :, :, tile * 128 : tile * 128 + 128].reshape(-1, 128) for q in range(4)
        ]
        for i in range(4):
            out = jnp.zeros_like(groups[0])
            for q in range(4):
                shift = (32 * (q - i)) % 128
                piece = pltpu.roll(groups[q], shift, 1) if shift else groups[q]
                out = jnp.where((lanes >> 5) == q, piece, out)
            in_out[tile * 4 + i] = out.astype(BF16).reshape(cols, rows // 4, frames, 128)


def shift_frames(x, by):
    zero = jnp.zeros_like(x[:, :1])
    if by > 0:
        return jnp.concatenate([zero, x[:, :-1]], axis=1)
    return jnp.concatenate([x[:, 1:], zero], axis=1)


def branch_kernel(
    pos, g0, g1, g2, g3, r0, r1, r2, r3, weight, own_out, left_out, right_out, ext
):
    cols, rows, frames, chans = g0.shape
    width = weight.shape[1]
    for k, (g, r) in enumerate(((g0, r0), (g1, r1), (g2, r2), (g3, r3))):
        ext[k, :, 1 : rows + 1] = g[...]
        ext[k, :, 0] = r[0]
        ext[k, :, rows + 1] = r[1]
    count = 4 * cols * rows * frames
    total = None
    for a in range(3):
        acc = jnp.zeros((count, 3 * width), F32)
        for b in range(3):
            lhs = ext[:, :, 2 - b : 2 - b + rows].reshape(count, chans)
            rhs = weight[9 * a + 3 * b : 9 * a + 3 * b + 3].reshape(3 * width, chans)
            acc = acc + lax.dot_general(
                lhs, rhs, (((1,), (1,)), ((), ())), preferred_element_type=F32
            )
        acc = acc.reshape(count // frames, frames, 3 * width)
        if a != 1:
            acc = shift_frames(acc, a - 1)
        total = acc if total is None else total + acc
    total = total.reshape(4, cols, rows, frames, 3 * width)
    for k in range(4):
        sample = lax.rem(pos[0] + (4 - k), 4)
        part = [[total[k, w, :, :, c * width : (c + 1) * width] for c in range(3)] for w in range(cols)]
        left_out[sample] = part[0][0].astype(BF16)
        own_out[sample, 0] = part[0][1] + part[1][0]
        own_out[sample, 1] = part[0][2] + part[1][1]
        right_out[sample] = part[1][2].astype(BF16)


def moment_kernel(chunks, proj, out, wide, flat):
    devices, cols, halves, frames, _ = chunks.shape
    across, rows, _, rank = proj.shape
    wide[0] = jnp.zeros_like(wide[0])
    wide[across + 1] = jnp.zeros_like(wide[0])
    wide[1 : across + 1] = proj[...]
    count = devices * cols * halves
    x = chunks[...].astype(F32).reshape(count, frames, 128)
    later = shift_frames(x, 1).reshape(count * frames, 128)
    sooner = shift_frames(x, -1).reshape(count * frames, 128)
    x = x.reshape(count * frames, 128)
    lanes = lax.broadcasted_iota(jnp.int32, x.shape, 1) >> 5
    acc = [None] * 9
    for q in range(4):
        lhs = jnp.zeros_like(x)
        for part, shift, block in ((later, (0 - 32 * q) % 128, 0), (x, (32 - 32 * q) % 128, 1), (sooner, (64 - 32 * q) % 128, 2)):
            moved = pltpu.roll(part, shift, 1) if shift else part
            lhs = jnp.where(lanes == block, moved, lhs)
        lhs = lhs.T.astype(BF16)
        for b in range(3):
            for c in range(3):
                low = 2 - b + 2 * q
                rhs = wide[2 - c : 2 - c + across, low : low + 2].reshape(count * frames, rank)
                y = jnp.dot(lhs, rhs, preferred_element_type=F32)
                acc[3 * b + c] = y if acc[3 * b + c] is None else acc[3 * b + c] + y
    for a in range(3):
        for j in range(2):
            for k in range(9):
                at = (27 * j + 9 * a + k) * 16
                flat[at : at + 16, :] = acc[k][(2 * a + j) * 16 : (2 * a + j) * 16 + 16, :]
    for m in range(16):
        out[m] = flat[pl.ds(m, 54, stride=16), :].astype(BF16)


def finish_kernel(up, parts, out, flat, outflat):
    frames, rows, cols, chans = up.shape
    _rows_to_scratch(up, flat)
    for tile in range(4):
        for w in range(cols):
            for h in range(rows):
                at = pl.ds(h * cols + w, frames, stride=rows * cols)
                outflat[tile, at, :] = flat[tile, at, :] + parts[tile, w, h].astype(F32)
    for t in range(frames):
        for h in range(rows):
            base = (t * rows + h) * cols
            row = [outflat[tile, base : base + cols, :] for tile in range(4)]
            out[t, h] = jnp.concatenate(row, axis=1).astype(BF16)


def ring(axis, shift):
    n = lax.axis_size(axis)
    return [(i, (i + shift) % n) for i in range(n)]


def line(axis, shift):
    n = lax.axis_size(axis)
    return [(i, i + shift) for i in range(n) if 0 <= i + shift < n]


def body(
    inputs, pre_activation, upstream, weight, first_moment, second_moment, hash_seed, step_count
):
    frames, rows, cols, chans = inputs.shape[1:]
    rank = first_moment.shape[1]
    tokens = frames * rows * cols
    sx = ("sxx", "sxz")
    g, proj, chunks, top, bot = _call(
        prepare,
        (
            jax.ShapeDtypeStruct((cols, rows, frames, chans), BF16),
            jax.ShapeDtypeStruct((cols, rows, frames, rank), BF16),
            jax.ShapeDtypeStruct((16, cols, 2, frames, 128), BF16),
            jax.ShapeDtypeStruct((cols, frames, chans + rank), BF16),
            jax.ShapeDtypeStruct((cols, frames, chans + rank), BF16),
        ),
        scratch=[pltpu.VMEM((chans // 128, tokens, 128), F32)] * 3,
        smem=1,
        total=4,
    )(hash_seed.reshape(1), pre_activation[0], upstream[0], inputs[0])

    above = lax.ppermute(bot, "sy", line("sy", 1))
    below = lax.ppermute(top, "sy", line("sy", -1))
    chunks = lax.all_to_all(chunks, sx, split_axis=0, concat_axis=0, tiled=True)
    g_all = [g] + [lax.ppermute(g, "dp", ring("dp", k)) for k in (1, 2, 3)]
    edge = jnp.stack([above[..., :chans], below[..., :chans]])
    edges = [edge] + [lax.ppermute(edge, "dp", ring("dp", k)) for k in (1, 2, 3)]
    proj = jnp.concatenate(
        [above[:, None, :, chans:], proj, below[:, None, :, chans:]], axis=1
    )
    proj = lax.all_to_all(
        jnp.broadcast_to(proj[None], (4,) + proj.shape), "sxz", 0, 0, tiled=True
    )
    proj = lax.all_to_all(
        jnp.broadcast_to(proj[None], (4,) + proj.shape), "sxx", 0, 0, tiled=True
    )
    proj = proj.reshape(16 * cols, rows + 2, frames, rank)
    terms = _call(
        moment_kernel,
        jax.ShapeDtypeStruct((16, 54, rank), BF16),
        scratch=[
            pltpu.VMEM((16 * cols + 2, rows + 2, frames, rank), BF16),
            pltpu.VMEM((54 * 16, rank), F32),
        ],
        total=2,
    )(chunks, proj)
    terms = lax.all_to_all(terms, ("dp", "sy"), 0, 0, tiled=True)

    place = lax.axis_index("dp").astype(jnp.int32).reshape(1)
    own, left, right = _call(
        branch_kernel,
        (
            jax.ShapeDtypeStruct((4, cols, rows, frames, 128), F32),
            jax.ShapeDtypeStruct((4, rows, frames, 128), BF16),
            jax.ShapeDtypeStruct((4, rows, frames, 128), BF16),
        ),
        scratch=[pltpu.VMEM((4, cols, rows + 2, frames, chans), BF16)],
        smem=1,
        total=10,
    )(place, *g_all, *edges, weight)
    from_right = lax.ppermute(left, sx, line(sx, -1))
    from_left = lax.ppermute(right, sx, line(sx, 1))
    mine = (own + jnp.stack([from_left, from_right], axis=1).astype(F32)).astype(BF16)
    parts = lax.all_to_all(mine, "dp", 0, 0, tiled=True)
    input_grad = _call(
        finish_kernel,
        jax.ShapeDtypeStruct((frames, rows, cols, chans), BF16),
        scratch=[pltpu.VMEM((chans // 128, tokens, 128), F32)] * 2,
        total=2,
    )(upstream[0], parts)

    total = 32768
    reduced = jnp.sum(terms.astype(F32), axis=0) / math.sqrt(total)
    new_first = 0.9 * first_moment + 0.1 * reduced
    new_second = 0.999 * second_moment + 0.001 * reduced * reduced
    step_value = step_count.astype(F32)
    first_bias = 1.0 - jnp.power(jnp.float32(0.9), step_value)
    second_bias = 1.0 - jnp.power(jnp.float32(0.999), step_value)
    adapted = new_first / first_bias / (jnp.sqrt(new_second / second_bias) + 1e-08)
    scales = jnp.sqrt(jnp.mean(adapted * adapted, axis=1)) / jnp.sqrt(
        jnp.mean(reduced * reduced, axis=1) + 1e-06
    )
    return (input_grad[None], new_first, new_second, scales)


def solution(mesh):
    sizes = mesh.shape
    grid = Mesh(
        mesh.devices.reshape(sizes["dp"], sizes["sy"], 4, sizes["sx"] // 4),
        ("dp", "sy", "sxx", "sxz"),
    )
    sx = ("sxx", "sxz")
    whole = ("dp", "sy", "sxx", "sxz")
    volume = P("dp", None, "sy", sx, None)
    return jax.shard_map(
        body,
        mesh=grid,
        in_specs=(volume, volume, volume, P(None, "dp", None), P(whole), P(whole), P(), P()),
        out_specs=(volume, P(whole), P(whole), P(whole)),
        check_vma=False,
    )
```

```python
import math

import jax
import jax.numpy as jnp
from jax import lax
from jax.experimental import pallas as pl
from jax.experimental.pallas import tpu as pltpu
from jax.sharding import Mesh, PartitionSpec as P

BF16 = jnp.bfloat16
F32 = jnp.float32


def _call(kernel, ins, outs, scratch=()):
    moved = [i for i, (_, space) in enumerate(ins) if space in ("hbm", "arg")]
    late = [i for i, (_, space) in enumerate(ins) if space == "late"]
    count = len(ins)

    def run(*refs):
        given = list(refs[:count])
        results = refs[count : count + len(outs)]
        rest = refs[count + len(outs) :]
        in_bufs = rest[: len(moved)]
        out_bufs = rest[len(moved) : len(moved) + len(outs)]
        late_bufs = rest[len(moved) + len(outs) :][: len(late)]
        own = rest[len(moved) + len(outs) + len(late) : -3]
        in_sem, late_sem, out_sem = rest[-3:]
        copies = []
        for n, i in enumerate(moved):
            copies.append(pltpu.make_async_copy(given[i], in_bufs[n], in_sem.at[n]))
            given[i] = in_bufs[n]
        for n, i in enumerate(late):
            third = given[i].shape[0] // 3
            pieces = [
                pltpu.make_async_copy(
                    given[i].at[pl.ds(a * third, third)],
                    late_bufs[n].at[pl.ds(a * third, third)],
                    late_sem.at[3 * n + a],
                )
                for a in range(3)
            ]
            for piece in pieces:
                piece.start()
            given[i] = (late_bufs[n], pieces)
        for copy in copies:
            copy.start()
        for copy in copies:
            copy.wait()
        kernel(*given, *out_bufs, *own)
        copies = [
            pltpu.make_async_copy(out_bufs[n], results[n], out_sem.at[n]) for n in range(len(outs))
        ]
        for copy in copies:
            copy.start()
        for copy in copies:
            copy.wait()

    buffers = [pltpu.VMEM(ins[i][0].shape, ins[i][0].dtype) for i in moved]
    buffers += [pltpu.VMEM(shape, dtype) for shape, dtype in outs]
    buffers += [pltpu.VMEM(ins[i][0].shape, ins[i][0].dtype) for i in late]
    arrays = [
        pltpu.with_memory_space_constraint(array, pltpu.HBM) if space in ("arg", "late") else array
        for array, space in ins
    ]
    return pl.pallas_call(
        run,
        out_shape=[jax.ShapeDtypeStruct(shape, dtype) for shape, dtype in outs],
        in_specs=[
            pl.BlockSpec(memory_space=pltpu.SMEM if space == "smem" else pltpu.HBM)
            for _, space in ins
        ],
        out_specs=[pl.BlockSpec(memory_space=pltpu.HBM) for _ in outs],
        scratch_shapes=buffers
        + list(scratch)
        + [
            pltpu.SemaphoreType.DMA((max(1, len(moved)),)),
            pltpu.SemaphoreType.DMA((max(1, 3 * len(late)),)),
            pltpu.SemaphoreType.DMA((len(outs),)),
        ],
        compiler_params=pltpu.CompilerParams(vmem_limit_bytes=40 * 1024 * 1024),
    )(*arrays)


def _rows_to_scratch(ref, scratch):
    frames, rows, cols, _ = ref.shape
    for t in range(frames):
        for h in range(rows):
            base = (t * rows + h) * cols
            row = ref[t, h].astype(F32)
            for tile in range(scratch.shape[0]):
                scratch[tile, base : base + cols, :] = row[:, tile * 128 : tile * 128 + 128]


def _token_major(scratch, frames, rows, cols):
    tiles = []
    for tile in range(scratch.shape[0]):
        tiles.append(
            jnp.concatenate(
                [
                    scratch[tile, pl.ds(h * cols + w, frames, stride=rows * cols), :]
                    for w in range(cols)
                    for h in range(rows)
                ],
                axis=0,
            )
        )
    return jnp.concatenate(tiles, axis=1)


def prepare(seed, pre, up, inp, g_out, proj_out, in_out, top_out, bot_out, s_pre, s_up, s_in):
    frames, rows, cols, chans = pre.shape
    rank = proj_out.shape[-1]
    _rows_to_scratch(pre, s_pre)
    _rows_to_scratch(up, s_up)
    _rows_to_scratch(inp, s_in)

    row_ids = lax.broadcasted_iota(jnp.int32, (chans, rank), 0)
    col_ids = lax.broadcasted_iota(jnp.int32, (chans, rank), 1)
    mixed = (row_ids * rank + col_ids) * jnp.int32(-1640531535) + seed[0] * jnp.int32(668265263)
    mixed = mixed ^ lax.shift_right_logical(mixed, jnp.int32(15))
    mixed = mixed * jnp.int32(-2048144777)
    mixed = mixed ^ lax.shift_right_logical(mixed, jnp.int32(13))
    mixed = mixed * jnp.int32(-1028477379)
    mixed = mixed ^ lax.shift_right_logical(mixed, jnp.int32(16))
    level = (lax.shift_right_logical(mixed, jnp.int32(8)) & jnp.int32(65535)).astype(F32)
    projector = (((level + 0.5) * (2.0 / 65536.0) - 1.0) * math.sqrt(3.0 / rank)).astype(BF16)

    x = _token_major(s_pre, frames, rows, cols)
    u = _token_major(s_up, frames, rows, cols)
    sig = jax.nn.sigmoid(x)
    g = (u * sig * (1.0 + x * (1.0 - sig))).astype(BF16)
    proj = jnp.dot(g, projector, preferred_element_type=F32).astype(BF16)
    g4 = g.reshape(cols, rows, frames, chans)
    p4 = proj.reshape(cols, rows, frames, rank)
    g_out[...] = g4
    proj_out[...] = p4
    top_out[:, :, :chans] = g4[:, 0]
    bot_out[:, :, :chans] = g4[:, rows - 1]
    top_out[:, :, chans:] = p4[:, 0]
    bot_out[:, :, chans:] = p4[:, rows - 1]

    dest = in_out.shape[0]
    r = lax.broadcasted_iota(jnp.int32, (chans, chans), 0)
    c = lax.broadcasted_iota(jnp.int32, (chans, chans), 1)
    target = (r & 1) * 16 + ((r >> 1) & 15) * 32 + (r >> 5)
    perm = jnp.where(c == target, 1.0, 0.0).astype(BF16)
    moved = jnp.dot(
        _token_major(s_in, frames, rows, cols).astype(BF16), perm, preferred_element_type=F32
    ).reshape(cols, 4, rows // 4, frames, chans)
    lanes = lax.broadcasted_iota(jnp.int32, (cols * (rows // 4) * frames, 128), 1)
    for tile in range(dest // 4):
        groups = [
            moved[:, q, :, :, tile * 128 : tile * 128 + 128].reshape(-1, 128) for q in range(4)
        ]
        for i in range(4):
            out = jnp.zeros_like(groups[0])
            for q in range(4):
                shift = (32 * (q - i)) % 128
                piece = pltpu.roll(groups[q], shift, 1) if shift else groups[q]
                out = jnp.where((lanes >> 5) == q, piece, out)
            in_out[tile * 4 + i] = out.astype(BF16).reshape(cols, rows // 4, frames, 128)


def assemble(pos, g, proj, chunks, above, below, g_out, *sends):
    _, rows, _, chans = g.shape
    depth = len(sends)
    top = jnp.where(pos[0] > 0, above[...], jnp.zeros_like(above[...]))
    bot = jnp.where(pos[0] < 3, below[...], jnp.zeros_like(below[...]))
    g_out[:, 1 : rows + 1] = g[...]
    g_out[:, 0] = top[:, :, :chans]
    g_out[:, rows + 1] = bot[:, :, :chans]
    for k, send in enumerate(sends):
        send[:, 1 : rows + 1] = proj[...]
        send[:, 0] = top[:, :, chans:]
        send[:, rows + 1] = bot[:, :, chans:]
        for x in range(chunks.shape[0] // depth):
            at = rows + 2 + 2 * x
            send[:, at : at + 2] = chunks[depth * x + lax.rem(pos[2] + k, depth)]


def across_x(pos, *refs):
    depth = len(refs) // 2
    along = depth
    rows = refs[0].shape[1] - 2 * along
    for m in range(along):
        send = refs[depth + m]
        at = rows + 2 * lax.rem(pos[1] + m, along)
        for k in range(depth):
            send[k, :, :rows] = refs[k][:, :rows]
            for w in range(refs[k].shape[0]):
                send[k, w, rows:] = refs[k][w, pl.ds(at, 2)]


def shift_frames(x, by):
    zero = jnp.zeros_like(x[:, :1])
    if by > 0:
        return jnp.concatenate([zero, x[:, :-1]], axis=1)
    return jnp.concatenate([x[:, 1:], zero], axis=1)


def branch_kernel(g0, g1, g2, g3, weight, own_out, left_out, right_out, ext):
    cols, rows, frames, chans = g0.shape
    rows = rows - 2
    weight, pieces = weight
    width = weight.shape[1]
    for k, g in enumerate((g0, g1, g2, g3)):
        ext[k] = g[...]
    count = 4 * cols * rows * frames
    total = None
    for a in range(3):
        pieces[a].wait()
        acc = jnp.zeros((count, 3 * width), F32)
        for b in range(3):
            lhs = ext[:, :, 2 - b : 2 - b + rows].reshape(count, chans)
            rhs = weight[9 * a + 3 * b : 9 * a + 3 * b + 3].reshape(3 * width, chans)
            acc = acc + lax.dot_general(
                lhs, rhs, (((1,), (1,)), ((), ())), preferred_element_type=F32
            )
        acc = acc.reshape(count // frames, frames, 3 * width)
        if a != 1:
            acc = shift_frames(acc, a - 1)
        total = acc if total is None else total + acc
    total = total.reshape(4, cols, rows, frames, 3 * width)
    for k in range(4):
        part = [[total[k, w, :, :, c * width : (c + 1) * width] for c in range(3)] for w in range(cols)]
        left_out[k] = part[0][0].astype(BF16)
        own_out[k, 0] = part[0][1] + part[1][0]
        own_out[k, 1] = part[0][2] + part[1][1]
        right_out[k] = part[1][2].astype(BF16)


def merge_kernel(pos, own, from_left, from_right, *outs):
    first = (pos[0] == 0) & (pos[1] == 0)
    last = (pos[0] == 3) & (pos[1] == 3)
    for k, out in enumerate(outs):
        left = from_left[k].astype(F32)
        right = from_right[k].astype(F32)
        out[0] = (own[k, 0] + jnp.where(first, 0.0, left)).astype(BF16)
        out[1] = (own[k, 1] + jnp.where(last, 0.0, right)).astype(BF16)


def moment_kernel(pos, g0, g1, g2, g3, out, wide, inner, flat):
    rows = wide.shape[1]
    depth, cols, _, frames, rank = g0.shape
    devices = 4 * depth
    halves = 2
    across = devices * cols
    for m, got in enumerate((g0, g1, g2, g3)):
        x_at = lax.rem(pos[0] + (4 - m), 4)
        for k in range(depth):
            at = depth * x_at + lax.rem(pos[1] + (depth - k), depth)
            inner[at] = got[k, :, rows:]
            for w in range(cols):
                wide[1 + cols * at + w] = got[k, w, :rows]
    wide[0] = jnp.zeros_like(wide[0])
    wide[across + 1] = jnp.zeros_like(wide[0])
    count = devices * cols * halves
    x = inner[...].astype(F32).reshape(count, frames, 128)
    later = shift_frames(x, 1).reshape(count * frames, 128)
    sooner = shift_frames(x, -1).reshape(count * frames, 128)
    x = x.reshape(count * frames, 128)
    lanes = lax.broadcasted_iota(jnp.int32, x.shape, 1) >> 5
    acc = [None] * 9
    for q in range(4):
        lhs = jnp.zeros_like(x)
        for part, shift, block in ((later, (0 - 32 * q) % 128, 0), (x, (32 - 32 * q) % 128, 1), (sooner, (64 - 32 * q) % 128, 2)):
            moved = pltpu.roll(part, shift, 1) if shift else part
            lhs = jnp.where(lanes == block, moved, lhs)
        lhs = lhs.T.astype(BF16)
        for b in range(3):
            for c in range(3):
                low = 2 - b + 2 * q
                rhs = wide[2 - c : 2 - c + across, low : low + 2].reshape(count * frames, rank)
                y = jnp.dot(lhs, rhs, preferred_element_type=F32)
                acc[3 * b + c] = y if acc[3 * b + c] is None else acc[3 * b + c] + y
    for a in range(3):
        for j in range(2):
            for k in range(9):
                at = (27 * j + 9 * a + k) * 16
                flat[at : at + 16, :] = acc[k][(2 * a + j) * 16 : (2 * a + j) * 16 + 16, :]
    for m in range(16):
        out[m] = flat[pl.ds(m, 54, stride=16), :].astype(BF16)


def finish_kernel(pos, up, p0, p1, p2, p3, out, flat, outflat):
    frames, rows, cols, _ = up.shape
    _rows_to_scratch(up, flat)
    for k, part in enumerate((p0, p1, p2, p3)):
        tile = lax.rem(pos[0] + k, 4)
        for w in range(cols):
            for h in range(rows):
                at = pl.ds(h * cols + w, frames, stride=rows * cols)
                outflat[tile, at, :] = flat[tile, at, :] + part[w, h].astype(F32)
    for t in range(frames):
        for h in range(rows):
            base = (t * rows + h) * cols
            row = [outflat[tile, base : base + cols, :] for tile in range(4)]
            out[t, h] = jnp.concatenate(row, axis=1).astype(BF16)


def ring(axis, shift):
    n = lax.axis_size(axis)
    return [(i, (i + shift) % n) for i in range(n)]


def around(arrays, axis, sign=1):
    got = list(arrays)
    for k in (1, 3, 2):
        got[k] = lax.ppermute(arrays[k], axis, ring(axis, sign * k))
    return got


def step(
    inputs, pre_activation, upstream, weight, first_moment, second_moment, hash_seed, step_count
):
    frames, rows, cols, chans = inputs.shape[1:]
    rank = first_moment.shape[1]
    tokens = frames * rows * cols
    sx = ("sxx", "sxz")
    spread = pltpu.VMEM((chans // 128, tokens, 128), F32)
    g, proj, chunks, top, bot = _call(
        prepare,
        [
            (hash_seed.reshape(1), "smem"),
            (pre_activation[0], "arg"),
            (upstream[0], "arg"),
            (inputs[0], "arg"),
        ],
        [
            ((cols, rows, frames, chans), BF16),
            ((cols, rows, frames, rank), BF16),
            ((16, cols, 2, frames, 128), BF16),
            ((cols, frames, chans + rank), BF16),
            ((cols, frames, chans + rank), BF16),
        ],
        [spread] * 3,
    )
    place = {a: lax.axis_index(a).astype(jnp.int32) for a in ("dp", "sy", "sxx", "sxz")}

    def places(*axes):
        return (jnp.stack([place[a] for a in axes]), "smem")

    above = lax.ppermute(bot, "sy", ring("sy", 1))
    below = lax.ppermute(top, "sy", ring("sy", -1))
    along_z = ((cols, rows + 2 + 8, frames, 128), BF16)
    along_x = ((4, cols, rows + 4, frames, 128), BF16)
    g, *sends = _call(
        assemble,
        [places("sy", "sxx", "sxz")]
        + [(a, "hbm") for a in (g, proj, chunks, above, below)],
        [((cols, rows + 2, frames, chans), BF16)] + [along_z] * 4,
    )
    got = around(sends, "sxz")
    sends = _call(
        across_x,
        [places("sy", "sxx", "sxz")] + [(a, "hbm") for a in got],
        [along_x] * 4,
    )
    got = around(sends, "sxx")
    g_all = around([g] * 4, "dp")
    (terms,) = _call(
        moment_kernel,
        [places("sxx", "sxz")] + [(a, "hbm") for a in got],
        [((16, 54, rank), BF16)],
        [
            pltpu.VMEM((16 * cols + 2, rows + 2, frames, rank), BF16),
            pltpu.VMEM((16, cols, 2, frames, 128), BF16),
            pltpu.VMEM((54 * 16, rank), F32),
        ],
    )
    terms = lax.all_to_all(terms, ("dp", "sy"), 0, 0, tiled=True)

    own, left, right = _call(
        branch_kernel,
        [(x, "hbm") for x in g_all] + [(weight, "late")],
        [
            ((4, cols, rows, frames, 128), F32),
            ((4, rows, frames, 128), BF16),
            ((4, rows, frames, 128), BF16),
        ],
        [pltpu.VMEM((4, cols, rows + 2, frames, chans), BF16)],
    )
    from_right = lax.ppermute(left, sx, ring(sx, -1))
    from_left = lax.ppermute(right, sx, ring(sx, 1))
    mine = _call(
        merge_kernel,
        [places("sxx", "sxz")] + [(a, "hbm") for a in (own, from_left, from_right)],
        [((cols, rows, frames, 128), BF16)] * 4,
    )
    parts = around(mine, "dp", -1)
    (input_grad,) = _call(
        finish_kernel,
        [places("dp"), (upstream[0], "arg")] + [(a, "hbm") for a in parts],
        [((frames, rows, cols, chans), BF16)],
        [spread] * 2,
    )

    total = 32768
    reduced = jnp.sum(terms.astype(F32), axis=0) / math.sqrt(total)
    new_first = 0.9 * first_moment + 0.1 * reduced
    new_second = 0.999 * second_moment + 0.001 * reduced * reduced
    step_value = step_count.astype(F32)
    first_bias = 1.0 - jnp.power(jnp.float32(0.9), step_value)
    second_bias = 1.0 - jnp.power(jnp.float32(0.999), step_value)
    adapted = new_first / first_bias / (jnp.sqrt(new_second / second_bias) + 1e-08)
    scales = jnp.sqrt(jnp.mean(adapted * adapted, axis=1)) / jnp.sqrt(
        jnp.mean(reduced * reduced, axis=1) + 1e-06
    )
    return (input_grad[None], new_first, new_second, scales)


def solution(mesh):
    sizes = mesh.shape
    grid = Mesh(
        mesh.devices.reshape(sizes["dp"], sizes["sy"], 4, sizes["sx"] // 4),
        ("dp", "sy", "sxx", "sxz"),
    )
    sx = ("sxx", "sxz")
    whole = ("dp", "sy", "sxx", "sxz")
    volume = P("dp", None, "sy", sx, None)
    return jax.shard_map(
        step,
        mesh=grid,
        in_specs=(volume, volume, volume, P(None, "dp", None), P(whole), P(whole), P(), P()),
        out_specs=(volume, P(whole), P(whole), P(whole)),
        check_vma=False,
    )
```

```python
import math

import jax
import jax.numpy as jnp
from jax import lax
from jax.experimental import pallas as pl
from jax.experimental.pallas import tpu as pltpu
from jax.sharding import Mesh, PartitionSpec as P

BF16 = jnp.bfloat16
F32 = jnp.float32


def _call(kernel, ins, outs, scratch=()):
    moved = [i for i, (_, space) in enumerate(ins) if space == "arg"]
    late = [i for i, (_, space) in enumerate(ins) if space == "late"]
    count = len(ins)

    def run(*refs):
        given = list(refs[:count])
        results = refs[count : count + len(outs)]
        rest = refs[count + len(outs) :]
        in_bufs = rest[: len(moved)]
        late_bufs = rest[len(moved) :][: len(late)]
        own = rest[len(moved) + len(late) : -2]
        in_sem, late_sem = rest[-2:]
        copies = []
        for n, i in enumerate(moved):
            copies.append(pltpu.make_async_copy(given[i], in_bufs[n], in_sem.at[n]))
            given[i] = in_bufs[n]
        for n, i in enumerate(late):
            third = given[i].shape[0] // 3
            pieces = [
                pltpu.make_async_copy(
                    given[i].at[pl.ds(a * third, third)],
                    late_bufs[n].at[pl.ds(a * third, third)],
                    late_sem.at[3 * n + a],
                )
                for a in range(3)
            ]
            for piece in pieces:
                piece.start()
            given[i] = (late_bufs[n], pieces)
        for copy in copies:
            copy.start()
        for copy in copies:
            copy.wait()
        kernel(*given, *results, *own)

    buffers = [pltpu.VMEM(ins[i][0].shape, ins[i][0].dtype) for i in moved]
    buffers += [pltpu.VMEM(ins[i][0].shape, ins[i][0].dtype) for i in late]
    arrays = [
        pltpu.with_memory_space_constraint(array, pltpu.HBM) if space in ("arg", "late") else array
        for array, space in ins
    ]
    return pl.pallas_call(
        run,
        out_shape=[jax.ShapeDtypeStruct(shape, dtype) for shape, dtype in outs],
        in_specs=[
            pl.BlockSpec(
                memory_space={"smem": pltpu.SMEM, "vmem": pltpu.VMEM}.get(space, pltpu.HBM)
            )
            for _, space in ins
        ],
        out_specs=[pl.BlockSpec(memory_space=pltpu.VMEM) for _ in outs],
        scratch_shapes=buffers
        + list(scratch)
        + [
            pltpu.SemaphoreType.DMA((max(1, len(moved)),)),
            pltpu.SemaphoreType.DMA((max(1, 3 * len(late)),)),
        ],
        compiler_params=pltpu.CompilerParams(vmem_limit_bytes=40 * 1024 * 1024),
    )(*arrays)


def _rows_to_scratch(ref, scratch):
    frames, rows, cols, _ = ref.shape
    for t in range(frames):
        for h in range(rows):
            base = (t * rows + h) * cols
            row = ref[t, h].astype(F32)
            for tile in range(scratch.shape[0]):
                scratch[tile, base : base + cols, :] = row[:, tile * 128 : tile * 128 + 128]


def _token_major(scratch, frames, rows, cols):
    tiles = []
    for tile in range(scratch.shape[0]):
        tiles.append(
            jnp.concatenate(
                [
                    scratch[tile, pl.ds(h * cols + w, frames, stride=rows * cols), :]
                    for w in range(cols)
                    for h in range(rows)
                ],
                axis=0,
            )
        )
    return jnp.concatenate(tiles, axis=1)


def prepare(seed, pre, up, inp, g_out, proj_out, in_out, top_out, bot_out, up_out, s_pre, s_up, s_in):
    frames, rows, cols, chans = pre.shape
    rank = proj_out.shape[-1]
    _rows_to_scratch(pre, s_pre)
    _rows_to_scratch(up, s_up)
    _rows_to_scratch(inp, s_in)

    row_ids = lax.broadcasted_iota(jnp.int32, (chans, rank), 0)
    col_ids = lax.broadcasted_iota(jnp.int32, (chans, rank), 1)
    mixed = (row_ids * rank + col_ids) * jnp.int32(-1640531535) + seed[0] * jnp.int32(668265263)
    mixed = mixed ^ lax.shift_right_logical(mixed, jnp.int32(15))
    mixed = mixed * jnp.int32(-2048144777)
    mixed = mixed ^ lax.shift_right_logical(mixed, jnp.int32(13))
    mixed = mixed * jnp.int32(-1028477379)
    mixed = mixed ^ lax.shift_right_logical(mixed, jnp.int32(16))
    level = (lax.shift_right_logical(mixed, jnp.int32(8)) & jnp.int32(65535)).astype(F32)
    projector = (((level + 0.5) * (2.0 / 65536.0) - 1.0) * math.sqrt(3.0 / rank)).astype(BF16)

    x = _token_major(s_pre, frames, rows, cols)
    u = _token_major(s_up, frames, rows, cols)
    sig = jax.nn.sigmoid(x)
    g = (u * sig * (1.0 + x * (1.0 - sig))).astype(BF16)
    proj = jnp.dot(g, projector, preferred_element_type=F32).astype(BF16)
    g4 = g.reshape(cols, rows, frames, chans)
    p4 = proj.reshape(cols, rows, frames, rank)
    g_out[...] = g4
    up_out[...] = u.astype(BF16).reshape(cols, rows, frames, chans)
    proj_out[...] = p4
    top_out[:, :, :chans] = g4[:, 0]
    bot_out[:, :, :chans] = g4[:, rows - 1]
    top_out[:, :, chans:] = p4[:, 0]
    bot_out[:, :, chans:] = p4[:, rows - 1]

    dest = in_out.shape[0]
    r = lax.broadcasted_iota(jnp.int32, (chans, chans), 0)
    c = lax.broadcasted_iota(jnp.int32, (chans, chans), 1)
    target = (r & 1) * 16 + ((r >> 1) & 15) * 32 + (r >> 5)
    perm = jnp.where(c == target, 1.0, 0.0).astype(BF16)
    moved = jnp.dot(
        _token_major(s_in, frames, rows, cols).astype(BF16), perm, preferred_element_type=F32
    ).reshape(cols, 4, rows // 4, frames, chans)
    lanes = lax.broadcasted_iota(jnp.int32, (cols * (rows // 4) * frames, 128), 1)
    for tile in range(dest // 4):
        groups = [
            moved[:, q, :, :, tile * 128 : tile * 128 + 128].reshape(-1, 128) for q in range(4)
        ]
        for i in range(4):
            out = jnp.zeros_like(groups[0])
            for q in range(4):
                shift = (32 * (q - i)) % 128
                piece = pltpu.roll(groups[q], shift, 1) if shift else groups[q]
                out = jnp.where((lanes >> 5) == q, piece, out)
            in_out[tile * 4 + i] = out.astype(BF16).reshape(cols, rows // 4, frames, 128)


def assemble(pos, g, proj, chunks, above, below, g_out, *sends):
    _, rows, _, chans = g.shape
    depth = len(sends)
    top = jnp.where(pos[0] > 0, above[...], jnp.zeros_like(above[...]))
    bot = jnp.where(pos[0] < 3, below[...], jnp.zeros_like(below[...]))
    g_out[:, 1 : rows + 1] = g[...]
    g_out[:, 0] = top[:, :, :chans]
    g_out[:, rows + 1] = bot[:, :, :chans]
    for k, send in enumerate(sends):
        send[:, 1 : rows + 1] = proj[...]
        send[:, 0] = top[:, :, chans:]
        send[:, rows + 1] = bot[:, :, chans:]
        for x in range(chunks.shape[0] // depth):
            at = rows + 2 + 2 * x
            send[:, at : at + 2] = chunks[depth * x + lax.rem(pos[2] + k, depth)]


def across_x(pos, *refs):
    depth = len(refs) // 2
    along = depth
    rows = refs[0].shape[1] - 2 * along
    for m in range(along):
        send = refs[depth + m]
        at = rows + 2 * lax.rem(pos[1] + m, along)
        for k in range(depth):
            send[k, :, :rows] = refs[k][:, :rows]
            for w in range(refs[k].shape[0]):
                send[k, w, rows:] = refs[k][w, pl.ds(at, 2)]


def shift_frames(x, by):
    zero = jnp.zeros_like(x[:, :1])
    if by > 0:
        return jnp.concatenate([zero, x[:, :-1]], axis=1)
    return jnp.concatenate([x[:, 1:], zero], axis=1)


def branch_kernel(g0, g1, g2, g3, weight, own_out, left_out, right_out, ext):
    cols, rows, frames, chans = g0.shape
    rows = rows - 2
    weight, pieces = weight
    width = weight.shape[1]
    for k, g in enumerate((g0, g1, g2, g3)):
        ext[k] = g[...]
    count = 4 * cols * rows * frames
    total = None
    for a in range(3):
        pieces[a].wait()
        acc = jnp.zeros((count, 3 * width), F32)
        for b in range(3):
            lhs = ext[:, :, 2 - b : 2 - b + rows].reshape(count, chans)
            rhs = weight[9 * a + 3 * b : 9 * a + 3 * b + 3].reshape(3 * width, chans)
            acc = acc + lax.dot_general(
                lhs, rhs, (((1,), (1,)), ((), ())), preferred_element_type=F32
            )
        acc = acc.reshape(count // frames, frames, 3 * width)
        if a != 1:
            acc = shift_frames(acc, a - 1)
        total = acc if total is None else total + acc
    total = total.reshape(4, cols, rows, frames, 3 * width)
    for k in range(4):
        part = [[total[k, w, :, :, c * width : (c + 1) * width] for c in range(3)] for w in range(cols)]
        left_out[k] = part[0][0].astype(BF16)
        own_out[k, 0] = part[0][1] + part[1][0]
        own_out[k, 1] = part[0][2] + part[1][1]
        right_out[k] = part[1][2].astype(BF16)


def merge_kernel(pos, own, from_left, from_right, *outs):
    first = (pos[0] == 0) & (pos[1] == 0)
    last = (pos[0] == 3) & (pos[1] == 3)
    for k, out in enumerate(outs):
        left = from_left[k].astype(F32)
        right = from_right[k].astype(F32)
        out[0] = (own[k, 0] + jnp.where(first, 0.0, left)).astype(BF16)
        out[1] = (own[k, 1] + jnp.where(last, 0.0, right)).astype(BF16)


def moment_kernel(pos, g0, g1, g2, g3, out, wide, inner, flat):
    rows = wide.shape[1]
    depth, cols, _, frames, rank = g0.shape
    devices = 4 * depth
    halves = 2
    across = devices * cols
    for m, got in enumerate((g0, g1, g2, g3)):
        x_at = lax.rem(pos[0] + (4 - m), 4)
        for k in range(depth):
            at = depth * x_at + lax.rem(pos[1] + (depth - k), depth)
            inner[at] = got[k, :, rows:]
            for w in range(cols):
                wide[1 + cols * at + w] = got[k, w, :rows]
    wide[0] = jnp.zeros_like(wide[0])
    wide[across + 1] = jnp.zeros_like(wide[0])
    count = devices * cols * halves
    x = inner[...].astype(F32).reshape(count, frames, 128)
    later = shift_frames(x, 1).reshape(count * frames, 128)
    sooner = shift_frames(x, -1).reshape(count * frames, 128)
    x = x.reshape(count * frames, 128)
    lanes = lax.broadcasted_iota(jnp.int32, x.shape, 1) >> 5
    acc = [None] * 9
    for q in range(4):
        lhs = jnp.zeros_like(x)
        for part, shift, block in ((later, (0 - 32 * q) % 128, 0), (x, (32 - 32 * q) % 128, 1), (sooner, (64 - 32 * q) % 128, 2)):
            moved = pltpu.roll(part, shift, 1) if shift else part
            lhs = jnp.where(lanes == block, moved, lhs)
        lhs = lhs.T.astype(BF16)
        for b in range(3):
            for c in range(3):
                low = 2 - b + 2 * q
                rhs = wide[2 - c : 2 - c + across, low : low + 2].reshape(count * frames, rank)
                y = jnp.dot(lhs, rhs, preferred_element_type=F32)
                acc[3 * b + c] = y if acc[3 * b + c] is None else acc[3 * b + c] + y
    for a in range(3):
        for j in range(2):
            for k in range(9):
                at = (27 * j + 9 * a + k) * 16
                flat[at : at + 16, :] = acc[k][(2 * a + j) * 16 : (2 * a + j) * 16 + 16, :]
    for m in range(16):
        out[m] = flat[pl.ds(m, 54, stride=16), :].astype(BF16)


def finish_kernel(pos, up, p0, p1, p2, p3, out, flat, outflat):
    cols, rows, frames, _ = up.shape
    for tile in range(4):
        flat[tile] = up[:, :, :, tile * 128 : tile * 128 + 128].astype(F32)
    for k, part in enumerate((p0, p1, p2, p3)):
        tile = lax.rem(pos[0] + k, 4)
        total = flat[tile] + part[...].astype(F32)
        for w in range(cols):
            for h in range(rows):
                outflat[tile, pl.ds(h * cols + w, frames, stride=rows * cols), :] = total[w, h]
    for t in range(frames):
        for h in range(rows):
            base = (t * rows + h) * cols
            row = [outflat[tile, base : base + cols, :] for tile in range(4)]
            out[t, h] = jnp.concatenate(row, axis=1).astype(BF16)


def ring(axis, shift):
    n = lax.axis_size(axis)
    return [(i, (i + shift) % n) for i in range(n)]


def around(arrays, axis, sign=1):
    got = list(arrays)
    for k in (1, 3, 2):
        got[k] = lax.ppermute(arrays[k], axis, ring(axis, sign * k))
    return got


def step(
    inputs, pre_activation, upstream, weight, first_moment, second_moment, hash_seed, step_count
):
    frames, rows, cols, chans = inputs.shape[1:]
    rank = first_moment.shape[1]
    tokens = frames * rows * cols
    sx = ("sxx", "sxz")
    spread = pltpu.VMEM((chans // 128, tokens, 128), F32)
    g, proj, chunks, top, bot, up = _call(
        prepare,
        [
            (hash_seed.reshape(1), "smem"),
            (pre_activation[0], "arg"),
            (upstream[0], "arg"),
            (inputs[0], "arg"),
        ],
        [
            ((cols, rows, frames, chans), BF16),
            ((cols, rows, frames, rank), BF16),
            ((16, cols, 2, frames, 128), BF16),
            ((cols, frames, chans + rank), BF16),
            ((cols, frames, chans + rank), BF16),
            ((cols, rows, frames, chans), BF16),
        ],
        [spread] * 3,
    )
    place = {a: lax.axis_index(a).astype(jnp.int32) for a in ("dp", "sy", "sxx", "sxz")}

    def places(*axes):
        return (jnp.stack([place[a] for a in axes]), "smem")

    above = lax.ppermute(bot, "sy", ring("sy", 1))
    below = lax.ppermute(top, "sy", ring("sy", -1))
    along_z = ((cols, rows + 2 + 8, frames, 128), BF16)
    along_x = ((4, cols, rows + 4, frames, 128), BF16)
    g, *sends = _call(
        assemble,
        [places("sy", "sxx", "sxz")]
        + [(a, "vmem") for a in (g, proj, chunks, above, below)],
        [((cols, rows + 2, frames, chans), BF16)] + [along_z] * 4,
    )
    got = around(sends, "sxz")
    sends = _call(
        across_x,
        [places("sy", "sxx", "sxz")] + [(a, "vmem") for a in got],
        [along_x] * 4,
    )
    got = around(sends, "sxx")
    g_all = around([g] * 4, "dp")
    (terms,) = _call(
        moment_kernel,
        [places("sxx", "sxz")] + [(a, "vmem") for a in got],
        [((16, 54, rank), BF16)],
        [
            pltpu.VMEM((16 * cols + 2, rows + 2, frames, rank), BF16),
            pltpu.VMEM((16, cols, 2, frames, 128), BF16),
            pltpu.VMEM((54 * 16, rank), F32),
        ],
    )
    terms = lax.all_to_all(terms, ("dp", "sy"), 0, 0, tiled=True)

    own, left, right = _call(
        branch_kernel,
        [(x, "vmem") for x in g_all] + [(weight, "late")],
        [
            ((4, cols, rows, frames, 128), F32),
            ((4, rows, frames, 128), BF16),
            ((4, rows, frames, 128), BF16),
        ],
        [pltpu.VMEM((4, cols, rows + 2, frames, chans), BF16)],
    )
    from_right = lax.ppermute(left, sx, ring(sx, -1))
    from_left = lax.ppermute(right, sx, ring(sx, 1))
    mine = _call(
        merge_kernel,
        [places("sxx", "sxz")] + [(a, "vmem") for a in (own, from_left, from_right)],
        [((cols, rows, frames, 128), BF16)] * 4,
    )
    parts = around(mine, "dp", -1)
    (input_grad,) = _call(
        finish_kernel,
        [places("dp"), (up, "vmem")] + [(a, "vmem") for a in parts],
        [((frames, rows, cols, chans), BF16)],
        [pltpu.VMEM((chans // 128, cols, rows, frames, 128), F32), spread],
    )

    total = 32768
    reduced = jnp.sum(terms.astype(F32), axis=0) / math.sqrt(total)
    new_first = 0.9 * first_moment + 0.1 * reduced
    new_second = 0.999 * second_moment + 0.001 * reduced * reduced
    step_value = step_count.astype(F32)
    first_bias = 1.0 - jnp.power(jnp.float32(0.9), step_value)
    second_bias = 1.0 - jnp.power(jnp.float32(0.999), step_value)
    adapted = new_first / first_bias / (jnp.sqrt(new_second / second_bias) + 1e-08)
    scales = jnp.sqrt(jnp.mean(adapted * adapted, axis=1)) / jnp.sqrt(
        jnp.mean(reduced * reduced, axis=1) + 1e-06
    )
    return (input_grad[None], new_first, new_second, scales)


def solution(mesh):
    sizes = mesh.shape
    grid = Mesh(
        mesh.devices.reshape(sizes["dp"], sizes["sy"], 4, sizes["sx"] // 4),
        ("dp", "sy", "sxx", "sxz"),
    )
    sx = ("sxx", "sxz")
    whole = ("dp", "sy", "sxx", "sxz")
    volume = P("dp", None, "sy", sx, None)
    return jax.shard_map(
        step,
        mesh=grid,
        in_specs=(volume, volume, volume, P(None, "dp", None), P(whole), P(whole), P(), P()),
        out_specs=(volume, P(whole), P(whole), P(whole)),
        check_vma=False,
    )
```

```python
import math

import jax
import jax.numpy as jnp
from jax import lax
from jax.experimental import pallas as pl
from jax.experimental.pallas import tpu as pltpu
from jax.sharding import Mesh, PartitionSpec as P

BF16 = jnp.bfloat16
F32 = jnp.float32
TOKENS = 32768


def _call(kernel, ins, outs, scratch=()):
    moved = [i for i, (_, space) in enumerate(ins) if space in ("arg", "scalar")]
    late = [i for i, (_, space) in enumerate(ins) if space == "late"]
    count = len(ins)

    def run(*refs):
        given = list(refs[:count])
        results = refs[count : count + len(outs)]
        rest = refs[count + len(outs) :]
        in_bufs = rest[: len(moved)]
        late_bufs = rest[len(moved) :][: len(late)]
        own = rest[len(moved) + len(late) : -2]
        in_sem, late_sem = rest[-2:]
        copies = []
        for n, i in enumerate(moved):
            copies.append(pltpu.make_async_copy(given[i], in_bufs[n], in_sem.at[n]))
            given[i] = in_bufs[n]
        for n, i in enumerate(late):
            pieces = [
                pltpu.make_async_copy(
                    given[i].at[pl.ds(9 * a + 3 * b, 3)],
                    late_bufs[n].at[b, pl.ds(3 * a, 3)],
                    late_sem.at[9 * n + 3 * b + a],
                )
                for b in range(3)
                for a in range(3)
            ]
            for piece in pieces[:6]:
                piece.start()
            given[i] = (late_bufs[n], pieces)
        for copy in copies:
            copy.start()
        for copy in copies:
            copy.wait()
        kernel(*given, *results, *own)

    buffers = [
        (pltpu.SMEM if ins[i][1] == "scalar" else pltpu.VMEM)(ins[i][0].shape, ins[i][0].dtype)
        for i in moved
    ]
    buffers += [pltpu.VMEM((3, 9) + ins[i][0].shape[1:], ins[i][0].dtype) for i in late]
    arrays = [
        pltpu.with_memory_space_constraint(array, pltpu.HBM) if space in ("arg", "late") else array
        for array, space in ins
    ]
    return pl.pallas_call(
        run,
        out_shape=[jax.ShapeDtypeStruct(shape, dtype) for shape, dtype in outs],
        in_specs=[
            pl.BlockSpec(
                memory_space={"smem": pltpu.SMEM, "vmem": pltpu.VMEM}.get(space, pltpu.HBM)
            )
            for _, space in ins
        ],
        out_specs=[pl.BlockSpec(memory_space=pltpu.VMEM) for _ in outs],
        scratch_shapes=buffers
        + list(scratch)
        + [
            pltpu.SemaphoreType.DMA((max(1, len(moved)),)),
            pltpu.SemaphoreType.DMA((max(1, 9 * len(late)),)),
        ],
        compiler_params=pltpu.CompilerParams(vmem_limit_bytes=40 * 1024 * 1024),
    )(*arrays)


def _rows_to_scratch(ref, scratch):
    frames, rows, cols, _ = ref.shape
    for t in range(frames):
        for h in range(rows):
            base = (t * rows + h) * cols
            row = ref[t, h].astype(F32)
            for tile in range(scratch.shape[0]):
                scratch[tile, base : base + cols, :] = row[:, tile * 128 : tile * 128 + 128]


def _token_major(scratch, frames, rows, cols):
    tiles = []
    for tile in range(scratch.shape[0]):
        tiles.append(
            jnp.concatenate(
                [
                    scratch[tile, pl.ds(h * cols + w, frames, stride=rows * cols), :]
                    for w in range(cols)
                    for h in range(rows)
                ],
                axis=0,
            )
        )
    return jnp.concatenate(tiles, axis=1)


def prepare(seed, pre, up, inp, g_out, proj_out, in_out, top_out, bot_out, up_out, s_pre, s_up, s_in):
    frames, rows, cols, chans = pre.shape
    rank = proj_out.shape[-1]
    _rows_to_scratch(pre, s_pre)
    _rows_to_scratch(up, s_up)
    _rows_to_scratch(inp, s_in)

    row_ids = lax.broadcasted_iota(jnp.int32, (chans, rank), 0)
    col_ids = lax.broadcasted_iota(jnp.int32, (chans, rank), 1)
    mixed = (row_ids * rank + col_ids) * jnp.int32(-1640531535) + seed[0] * jnp.int32(668265263)
    mixed = mixed ^ lax.shift_right_logical(mixed, jnp.int32(15))
    mixed = mixed * jnp.int32(-2048144777)
    mixed = mixed ^ lax.shift_right_logical(mixed, jnp.int32(13))
    mixed = mixed * jnp.int32(-1028477379)
    mixed = mixed ^ lax.shift_right_logical(mixed, jnp.int32(16))
    level = (lax.shift_right_logical(mixed, jnp.int32(8)) & jnp.int32(65535)).astype(F32)
    projector = (((level + 0.5) * (2.0 / 65536.0) - 1.0) * math.sqrt(3.0 / rank)).astype(BF16)

    x = _token_major(s_pre, frames, rows, cols)
    u = _token_major(s_up, frames, rows, cols)
    sig = jax.nn.sigmoid(x)
    g = (u * sig * (1.0 + x * (1.0 - sig))).astype(BF16)
    proj = jnp.dot(g, projector, preferred_element_type=F32).astype(BF16)
    g4 = g.reshape(cols, rows, frames, chans)
    p4 = proj.reshape(cols, rows, frames, rank)
    g_out[...] = g4
    up_out[...] = u.astype(BF16).reshape(cols, rows, frames, chans)
    proj_out[...] = p4
    top_out[:, :, :chans] = g4[:, 0]
    bot_out[:, :, :chans] = g4[:, rows - 1]
    top_out[:, :, chans:] = p4[:, 0]
    bot_out[:, :, chans:] = p4[:, rows - 1]

    dest = in_out.shape[0]
    r = lax.broadcasted_iota(jnp.int32, (chans, chans), 0)
    c = lax.broadcasted_iota(jnp.int32, (chans, chans), 1)
    target = (r & 1) * 16 + ((r >> 1) & 15) * 32 + (r >> 5)
    perm = jnp.where(c == target, 1.0, 0.0).astype(BF16)
    moved = jnp.dot(
        _token_major(s_in, frames, rows, cols).astype(BF16), perm, preferred_element_type=F32
    ).reshape(cols, 4, rows // 4, frames, chans)
    lanes = lax.broadcasted_iota(jnp.int32, (cols * (rows // 4) * frames, 128), 1)
    for tile in range(dest // 4):
        groups = [
            moved[:, q, :, :, tile * 128 : tile * 128 + 128].reshape(-1, 128) for q in range(4)
        ]
        for i in range(4):
            out = jnp.zeros_like(groups[0])
            for q in range(4):
                shift = (32 * (q - i)) % 128
                piece = pltpu.roll(groups[q], shift, 1) if shift else groups[q]
                out = jnp.where((lanes >> 5) == q, piece, out)
            in_out[tile * 4 + i] = out.astype(BF16).reshape(cols, rows // 4, frames, 128)


def assemble(at_y, at_z, g, proj, chunks, above, below, g_out, *sends):
    _, rows, _, chans = g.shape
    depth = len(sends)
    top = jnp.where(at_y[0] > 0, above[...], jnp.zeros_like(above[...]))
    bot = jnp.where(at_y[0] < 3, below[...], jnp.zeros_like(below[...]))
    g_out[:, 1 : rows + 1] = g[...]
    g_out[:, 0] = top[:, :, :chans]
    g_out[:, rows + 1] = bot[:, :, :chans]
    for k, send in enumerate(sends):
        send[:, 1 : rows + 1] = proj[...]
        send[:, 0] = top[:, :, chans:]
        send[:, rows + 1] = bot[:, :, chans:]
        for x in range(chunks.shape[0] // depth):
            at = rows + 2 + 2 * x
            send[:, at : at + 2] = chunks[depth * x + lax.rem(at_z[0] + k, depth)]


def across_x(at_x, *refs):
    depth = len(refs) // 2
    along = depth
    rows = refs[0].shape[1] - 2 * along
    for m in range(along):
        send = refs[depth + m]
        at = rows + 2 * lax.rem(at_x[0] + m, along)
        for k in range(depth):
            send[k, :, :rows] = refs[k][:, :rows]
            for w in range(refs[k].shape[0]):
                send[k, w, rows:] = refs[k][w, pl.ds(at, 2)]


def shift_frames(x, by):
    zero = jnp.zeros_like(x[:, :1])
    if by > 0:
        return jnp.concatenate([zero, x[:, :-1]], axis=1)
    return jnp.concatenate([x[:, 1:], zero], axis=1)


def branch_kernel(g0, g1, g2, g3, weight, own_out, left_out, right_out, ext):
    cols, rows, frames, chans = g0.shape
    rows = rows - 2
    weight, pieces = weight
    width = weight.shape[2]
    for k, g in enumerate((g0, g1, g2, g3)):
        ext[k] = g[...]
    count = 4 * cols * rows * frames
    acc = None
    for b in range(3):
        for piece in pieces[3 * b : 3 * b + 3]:
            piece.wait()
        if b == 0:
            for piece in pieces[6:]:
                piece.start()
        lhs = ext[:, :, 2 - b : 2 - b + rows].reshape(count, chans)
        y = lax.dot_general(
            lhs,
            weight[b].reshape(9 * width, chans),
            (((1,), (1,)), ((), ())),
            preferred_element_type=F32,
        )
        acc = y if acc is None else acc + y
    acc = acc.reshape(count // frames, frames, 9 * width)
    total = (
        shift_frames(acc[:, :, : 3 * width], -1)
        + acc[:, :, 3 * width : 6 * width]
        + shift_frames(acc[:, :, 6 * width :], 1)
    )
    total = total.reshape(4, cols, rows, frames, 3 * width)
    for k in range(4):
        part = [[total[k, w, :, :, c * width : (c + 1) * width] for c in range(3)] for w in range(cols)]
        left_out[k] = part[0][0].astype(BF16)
        own_out[k, 0] = part[0][1] + part[1][0]
        own_out[k, 1] = part[0][2] + part[1][1]
        right_out[k] = part[1][2].astype(BF16)


def merge_kernel(at_x, at_z, own, from_left, from_right, *outs):
    first = (at_x[0] == 0) & (at_z[0] == 0)
    last = (at_x[0] == 3) & (at_z[0] == 3)
    for k, out in enumerate(outs):
        left = from_left[k].astype(F32)
        right = from_right[k].astype(F32)
        out[0] = (own[k, 0] + jnp.where(first, 0.0, left)).astype(BF16)
        out[1] = (own[k, 1] + jnp.where(last, 0.0, right)).astype(BF16)


def moment_kernel(at_x, at_z, g0, g1, g2, g3, out, wide, inner, flat):
    rows = wide.shape[1]
    depth, cols, _, frames, rank = g0.shape
    devices = 4 * depth
    halves = 2
    across = devices * cols
    for m, got in enumerate((g0, g1, g2, g3)):
        x_at = lax.rem(at_x[0] + (4 - m), 4)
        for k in range(depth):
            at = depth * x_at + lax.rem(at_z[0] + (depth - k), depth)
            inner[at] = got[k, :, rows:]
            for w in range(cols):
                wide[1 + cols * at + w] = got[k, w, :rows]
    wide[0] = jnp.zeros_like(wide[0])
    wide[across + 1] = jnp.zeros_like(wide[0])
    count = devices * cols * halves
    x = inner[...].astype(F32).reshape(count, frames, 128)
    later = shift_frames(x, 1).reshape(count * frames, 128)
    sooner = shift_frames(x, -1).reshape(count * frames, 128)
    x = x.reshape(count * frames, 128)
    lanes = lax.broadcasted_iota(jnp.int32, x.shape, 1) >> 5
    acc = None
    for q in range(4):
        lhs = jnp.zeros_like(x)
        for part, shift, block in ((later, (0 - 32 * q) % 128, 0), (x, (32 - 32 * q) % 128, 1), (sooner, (64 - 32 * q) % 128, 2)):
            moved = pltpu.roll(part, shift, 1) if shift else part
            lhs = jnp.where(lanes == block, moved, lhs)
        lhs = lhs.T.astype(BF16)
        rhs = jnp.concatenate(
            [
                wide[2 - c : 2 - c + across, 2 - b + 2 * q : 4 - b + 2 * q].reshape(
                    count * frames, rank
                )
                for b in range(3)
                for c in range(3)
            ],
            axis=1,
        )
        y = jnp.dot(lhs, rhs, preferred_element_type=F32)
        acc = y if acc is None else acc + y
    for a in range(3):
        for j in range(2):
            for k in range(9):
                at = (27 * j + 9 * a + k) * 16
                flat[at : at + 16, :] = acc[
                    (2 * a + j) * 16 : (2 * a + j) * 16 + 16, k * rank : (k + 1) * rank
                ]
    for m in range(16):
        out[m] = flat[pl.ds(m, 54, stride=16), :].astype(BF16)


def owner_kernel(step, terms, first, second, first_out, second_out, scales_out):
    reduced = terms[0].astype(F32)
    for k in range(1, terms.shape[0]):
        reduced = reduced + terms[k].astype(F32)
    reduced = reduced * (1.0 / math.sqrt(TOKENS))
    new_first = 0.9 * first[...] + 0.1 * reduced
    new_second = 0.999 * second[...] + 0.001 * (reduced * reduced)
    count = jnp.full((1, 128), step[0], jnp.int32).astype(F32)
    first_bias = 1.0 - jnp.power(jnp.float32(0.9), count)
    second_bias = 1.0 - jnp.power(jnp.float32(0.999), count)
    adapted = new_first / first_bias / (jnp.sqrt(new_second / second_bias) + 1e-08)
    first_out[...] = new_first
    second_out[...] = new_second
    rest = jnp.zeros((128 - reduced.shape[0], 128), F32)

    def row_means(x):
        square = jnp.concatenate([x * x, rest], axis=0)
        return jnp.mean(square.T, axis=0, keepdims=True)

    scales = jnp.sqrt(row_means(adapted)) / jnp.sqrt(row_means(reduced) + 1e-06)
    scales_out[...] = scales[0, : reduced.shape[0]]


def finish_kernel(at_d, up, p0, p1, p2, p3, out, flat, outflat):
    cols, rows, frames, _ = up.shape
    for tile in range(4):
        flat[tile] = up[:, :, :, tile * 128 : tile * 128 + 128].astype(F32)
    for k, part in enumerate((p0, p1, p2, p3)):
        tile = lax.rem(at_d[0] + k, 4)
        total = flat[tile] + part[...].astype(F32)
        for w in range(cols):
            for h in range(rows):
                outflat[tile, pl.ds(h * cols + w, frames, stride=rows * cols), :] = total[w, h]
    for t in range(frames):
        for h in range(rows):
            base = (t * rows + h) * cols
            row = [outflat[tile, base : base + cols, :] for tile in range(4)]
            out[t, h] = jnp.concatenate(row, axis=1).astype(BF16)


def ring(axis, shift):
    n = lax.axis_size(axis)
    return [(i, (i + shift) % n) for i in range(n)]


def around(arrays, axis, sign=1):
    got = list(arrays)
    for k in (1, 3, 2):
        got[k] = lax.ppermute(arrays[k], axis, ring(axis, sign * k))
    return got


def step(
    inputs, pre_activation, upstream, weight, first_moment, second_moment, hash_seed, step_count
):
    frames, rows, cols, chans = inputs.shape[1:]
    rank = first_moment.shape[1]
    tokens = frames * rows * cols
    sx = ("sxx", "sxz")
    spread = pltpu.VMEM((chans // 128, tokens, 128), F32)
    g, proj, chunks, top, bot, up = _call(
        prepare,
        [
            (hash_seed.reshape(1), "scalar"),
            (pre_activation[0], "arg"),
            (upstream[0], "arg"),
            (inputs[0], "arg"),
        ],
        [
            ((cols, rows, frames, chans), BF16),
            ((cols, rows, frames, rank), BF16),
            ((16, cols, 2, frames, 128), BF16),
            ((cols, frames, chans + rank), BF16),
            ((cols, frames, chans + rank), BF16),
            ((cols, rows, frames, chans), BF16),
        ],
        [spread] * 3,
    )
    place = {a: lax.axis_index(a).astype(jnp.int32) for a in ("dp", "sy", "sxx", "sxz")}

    def places(*axes):
        return [(place[a].reshape(1), "smem") for a in axes]

    above = lax.ppermute(bot, "sy", ring("sy", 1))
    below = lax.ppermute(top, "sy", ring("sy", -1))
    along_z = ((cols, rows + 2 + 8, frames, 128), BF16)
    along_x = ((4, cols, rows + 4, frames, 128), BF16)
    g, *sends = _call(
        assemble,
        places("sy", "sxz")
        + [(a, "vmem") for a in (g, proj, chunks, above, below)],
        [((cols, rows + 2, frames, chans), BF16)] + [along_z] * 4,
    )
    got = around(sends, "sxz")
    sends = _call(
        across_x,
        places("sxx") + [(a, "vmem") for a in got],
        [along_x] * 4,
    )
    got = around(sends, "sxx")
    g_all = around([g] * 4, "dp")
    (terms,) = _call(
        moment_kernel,
        places("sxx", "sxz") + [(a, "vmem") for a in got],
        [((16, 54, rank), BF16)],
        [
            pltpu.VMEM((16 * cols + 2, rows + 2, frames, rank), BF16),
            pltpu.VMEM((16, cols, 2, frames, 128), BF16),
            pltpu.VMEM((54 * 16, rank), F32),
        ],
    )
    terms = lax.all_to_all(terms, ("dp", "sy"), 0, 0, tiled=True)

    own, left, right = _call(
        branch_kernel,
        [(x, "vmem") for x in g_all] + [(weight, "late")],
        [
            ((4, cols, rows, frames, 128), F32),
            ((4, rows, frames, 128), BF16),
            ((4, rows, frames, 128), BF16),
        ],
        [pltpu.VMEM((4, cols, rows + 2, frames, chans), BF16)],
    )
    from_right = lax.ppermute(left, sx, ring(sx, -1))
    from_left = lax.ppermute(right, sx, ring(sx, 1))
    mine = _call(
        merge_kernel,
        places("sxx", "sxz") + [(a, "vmem") for a in (own, from_left, from_right)],
        [((cols, rows, frames, 128), BF16)] * 4,
    )
    parts = around(mine, "dp", -1)
    (input_grad,) = _call(
        finish_kernel,
        places("dp") + [(up, "vmem")] + [(a, "vmem") for a in parts],
        [((frames, rows, cols, chans), BF16)],
        [pltpu.VMEM((chans // 128, cols, rows, frames, 128), F32), spread],
    )

    new_first, new_second, scales = _call(
        owner_kernel,
        [(step_count.reshape(1), "scalar")]
        + [(a, "vmem") for a in (terms, first_moment, second_moment)],
        [(first_moment.shape, F32), (first_moment.shape, F32), ((first_moment.shape[0],), F32)],
    )
    return (input_grad[None], new_first, new_second, scales)


def solution(mesh):
    sizes = mesh.shape
    grid = Mesh(
        mesh.devices.reshape(sizes["dp"], sizes["sy"], 4, sizes["sx"] // 4),
        ("dp", "sy", "sxx", "sxz"),
    )
    sx = ("sxx", "sxz")
    whole = ("dp", "sy", "sxx", "sxz")
    volume = P("dp", None, "sy", sx, None)
    return jax.shard_map(
        step,
        mesh=grid,
        in_specs=(volume, volume, volume, P(None, "dp", None), P(whole), P(whole), P(), P()),
        out_specs=(volume, P(whole), P(whole), P(whole)),
        check_vma=False,
    )
```

```python
import math

import jax
import jax.numpy as jnp
from jax import lax
from jax.experimental import pallas as pl
from jax.experimental.pallas import tpu as pltpu
from jax.sharding import Mesh, PartitionSpec as P

BF16 = jnp.bfloat16
F32 = jnp.float32
TOKENS = 32768


def _call(kernel, ins, outs, scratch=()):
    moved = [i for i, (_, space) in enumerate(ins) if space in ("arg", "scalar")]
    late = [i for i, (_, space) in enumerate(ins) if space == "late"]
    count = len(ins)

    def run(*refs):
        given = list(refs[:count])
        results = refs[count : count + len(outs)]
        rest = refs[count + len(outs) :]
        in_bufs = rest[: len(moved)]
        late_bufs = rest[len(moved) :][: len(late)]
        sems = rest[len(rest) - bool(moved) - bool(late) :]
        own = rest[len(moved) + len(late) : len(rest) - len(sems)]
        in_sem, late_sem = sems[0] if moved else None, sems[-1] if late else None
        copies = []
        for n, i in enumerate(moved):
            copies.append(pltpu.make_async_copy(given[i], in_bufs[n], in_sem.at[n]))
            given[i] = in_bufs[n]
        for n, i in enumerate(late):
            pieces = [
                pltpu.make_async_copy(
                    given[i].at[pl.ds(9 * a + 3 * b, 3)],
                    late_bufs[n].at[b, pl.ds(3 * a, 3)],
                    late_sem.at[9 * n + 3 * b + a],
                )
                for b in range(3)
                for a in range(3)
            ]
            for at, piece in enumerate(pieces):
                piece.start(priority=at % 2)
            given[i] = (late_bufs[n], pieces)
        for copy in copies:
            copy.start()
        for copy in copies:
            copy.wait()
        kernel(*given, *results, *own)

    buffers = [
        (pltpu.SMEM if ins[i][1] == "scalar" else pltpu.VMEM)(ins[i][0].shape, ins[i][0].dtype)
        for i in moved
    ]
    buffers += [pltpu.VMEM((3, 9) + ins[i][0].shape[1:], ins[i][0].dtype) for i in late]
    arrays = [
        pltpu.with_memory_space_constraint(array, pltpu.HBM) if space in ("arg", "late") else array
        for array, space in ins
    ]
    return pl.pallas_call(
        run,
        out_shape=[jax.ShapeDtypeStruct(shape, dtype) for shape, dtype in outs],
        in_specs=[
            pl.BlockSpec(
                memory_space={"smem": pltpu.SMEM, "vmem": pltpu.VMEM}.get(space, pltpu.HBM)
            )
            for _, space in ins
        ],
        out_specs=[pl.BlockSpec(memory_space=pltpu.VMEM) for _ in outs],
        scratch_shapes=buffers
        + list(scratch)
        + [pltpu.SemaphoreType.DMA((n,)) for n in (len(moved), 9 * len(late)) if n],
        compiler_params=pltpu.CompilerParams(vmem_limit_bytes=40 * 1024 * 1024),
    )(*arrays)


def _rows_to_scratch(ref, scratch):
    frames, rows, cols, _ = ref.shape
    for t in range(frames):
        for h in range(rows):
            base = (t * rows + h) * cols
            row = ref[t, h].astype(F32)
            for tile in range(scratch.shape[0]):
                scratch[tile, base : base + cols, :] = row[:, tile * 128 : tile * 128 + 128]


def _token_major(scratch, frames, rows, cols):
    tiles = []
    for tile in range(scratch.shape[0]):
        tiles.append(
            jnp.concatenate(
                [
                    scratch[tile, pl.ds(h * cols + w, frames, stride=rows * cols), :]
                    for w in range(cols)
                    for h in range(rows)
                ],
                axis=0,
            )
        )
    return jnp.concatenate(tiles, axis=1)


def prepare(seed, pre, up, g_out, proj_out, top_out, bot_out, up_out, s_pre, s_up):
    frames, rows, cols, chans = pre.shape
    rank = proj_out.shape[-1]
    _rows_to_scratch(pre, s_pre)
    _rows_to_scratch(up, s_up)

    row_ids = lax.broadcasted_iota(jnp.int32, (chans, rank), 0)
    col_ids = lax.broadcasted_iota(jnp.int32, (chans, rank), 1)
    mixed = (row_ids * rank + col_ids) * jnp.int32(-1640531535) + seed[0] * jnp.int32(668265263)
    mixed = mixed ^ lax.shift_right_logical(mixed, jnp.int32(15))
    mixed = mixed * jnp.int32(-2048144777)
    mixed = mixed ^ lax.shift_right_logical(mixed, jnp.int32(13))
    mixed = mixed * jnp.int32(-1028477379)
    mixed = mixed ^ lax.shift_right_logical(mixed, jnp.int32(16))
    level = (lax.shift_right_logical(mixed, jnp.int32(8)) & jnp.int32(65535)).astype(F32)
    projector = (((level + 0.5) * (2.0 / 65536.0) - 1.0) * math.sqrt(3.0 / rank)).astype(BF16)

    x = _token_major(s_pre, frames, rows, cols)
    u = _token_major(s_up, frames, rows, cols)
    sig = jax.nn.sigmoid(x)
    g = (u * sig * (1.0 + x * (1.0 - sig))).astype(BF16)
    proj = jnp.dot(g, projector, preferred_element_type=F32).astype(BF16)
    g4 = g.reshape(cols, rows, frames, chans)
    p4 = proj.reshape(cols, rows, frames, rank)
    g_out[...] = g4
    up_out[...] = u.astype(BF16).reshape(cols, rows, frames, chans)
    proj_out[...] = p4
    top_out[:, :, :chans] = g4[:, 0]
    bot_out[:, :, :chans] = g4[:, rows - 1]
    top_out[:, :, chans:] = p4[:, 0]
    bot_out[:, :, chans:] = p4[:, rows - 1]


def pack_inputs(inp, in_out, s_in):
    frames, rows, cols, chans = inp.shape
    _rows_to_scratch(inp, s_in)
    dest = in_out.shape[0]
    r = lax.broadcasted_iota(jnp.int32, (chans, chans), 0)
    c = lax.broadcasted_iota(jnp.int32, (chans, chans), 1)
    target = (r & 1) * 16 + ((r >> 1) & 15) * 32 + (r >> 5)
    perm = jnp.where(c == target, 1.0, 0.0).astype(BF16)
    moved = jnp.dot(
        _token_major(s_in, frames, rows, cols).astype(BF16), perm, preferred_element_type=F32
    ).reshape(cols, 4, rows // 4, frames, chans)
    lanes = lax.broadcasted_iota(jnp.int32, (cols * (rows // 4) * frames, 128), 1)
    for tile in range(dest // 4):
        groups = [
            moved[:, q, :, :, tile * 128 : tile * 128 + 128].reshape(-1, 128) for q in range(4)
        ]
        for i in range(4):
            out = jnp.zeros_like(groups[0])
            for q in range(4):
                shift = (32 * (q - i)) % 128
                piece = pltpu.roll(groups[q], shift, 1) if shift else groups[q]
                out = jnp.where((lanes >> 5) == q, piece, out)
            in_out[tile * 4 + i] = out.astype(BF16).reshape(cols, rows // 4, frames, 128)


def assemble(at_y, at_z, g, proj, chunks, above, below, g_out, *sends):
    _, rows, _, chans = g.shape
    depth = len(sends)
    top = jnp.where(at_y[0] > 0, above[...], jnp.zeros_like(above[...]))
    bot = jnp.where(at_y[0] < 3, below[...], jnp.zeros_like(below[...]))
    g_out[:, 1 : rows + 1] = g[...]
    g_out[:, 0] = top[:, :, :chans]
    g_out[:, rows + 1] = bot[:, :, :chans]
    for k, send in enumerate(sends):
        send[:, 1 : rows + 1] = proj[...]
        send[:, 0] = top[:, :, chans:]
        send[:, rows + 1] = bot[:, :, chans:]
        for x in range(chunks.shape[0] // depth):
            at = rows + 2 + 2 * x
            send[:, at : at + 2] = chunks[depth * x + lax.rem(at_z[0] + k, depth)]


def across_x(at_x, *refs):
    depth = len(refs) // 2
    along = depth
    rows = refs[0].shape[1] - 2 * along
    for m in range(along):
        send = refs[depth + m]
        at = rows + 2 * lax.rem(at_x[0] + m, along)
        for k in range(depth):
            send[k, :, :rows] = refs[k][:, :rows]
            for w in range(refs[k].shape[0]):
                send[k, w, rows:] = refs[k][w, pl.ds(at, 2)]


def shift_frames(x, by):
    zero = jnp.zeros_like(x[:, :1])
    if by > 0:
        return jnp.concatenate([zero, x[:, :-1]], axis=1)
    return jnp.concatenate([x[:, 1:], zero], axis=1)


def branch_kernel(g0, g1, g2, g3, weight, own_out, left_out, right_out, ext):
    cols, rows, frames, chans = g0.shape
    rows = rows - 2
    weight, pieces = weight
    width = weight.shape[2]
    for k, g in enumerate((g0, g1, g2, g3)):
        ext[k] = g[...]
    count = 4 * cols * rows * frames
    acc = None
    for b in range(3):
        for piece in pieces[3 * b : 3 * b + 3]:
            piece.wait()
        lhs = ext[:, :, 2 - b : 2 - b + rows].reshape(count, chans)
        y = lax.dot_general(
            lhs,
            weight[b].reshape(9 * width, chans),
            (((1,), (1,)), ((), ())),
            preferred_element_type=F32,
        )
        acc = y if acc is None else acc + y
    acc = acc.reshape(count // frames, frames, 9 * width)
    total = (
        shift_frames(acc[:, :, : 3 * width], -1)
        + acc[:, :, 3 * width : 6 * width]
        + shift_frames(acc[:, :, 6 * width :], 1)
    )
    total = total.reshape(4, cols, rows, frames, 3 * width)
    for k in range(4):
        part = [[total[k, w, :, :, c * width : (c + 1) * width] for c in range(3)] for w in range(cols)]
        left_out[k] = part[0][0].astype(BF16)
        own_out[k, 0] = part[0][1] + part[1][0]
        own_out[k, 1] = part[0][2] + part[1][1]
        right_out[k] = part[1][2].astype(BF16)


def merge_kernel(at_x, at_z, own, from_left, from_right, *outs):
    first = (at_x[0] == 0) & (at_z[0] == 0)
    last = (at_x[0] == 3) & (at_z[0] == 3)
    for k, out in enumerate(outs):
        left = from_left[k].astype(F32)
        right = from_right[k].astype(F32)
        out[0] = (own[k, 0] + jnp.where(first, 0.0, left)).astype(BF16)
        out[1] = (own[k, 1] + jnp.where(last, 0.0, right)).astype(BF16)


def moment_kernel(at_x, at_z, g0, g1, g2, g3, out, wide, inner, flat):
    rows = wide.shape[1]
    depth, cols, _, frames, rank = g0.shape
    devices = 4 * depth
    halves = 2
    across = devices * cols
    for m, got in enumerate((g0, g1, g2, g3)):
        x_at = lax.rem(at_x[0] + (4 - m), 4)
        for k in range(depth):
            at = depth * x_at + lax.rem(at_z[0] + (depth - k), depth)
            inner[at] = got[k, :, rows:]
            for w in range(cols):
                wide[1 + cols * at + w] = got[k, w, :rows]
    wide[0] = jnp.zeros_like(wide[0])
    wide[across + 1] = jnp.zeros_like(wide[0])
    count = devices * cols * halves
    x = inner[...].astype(F32).reshape(count, frames, 128)
    later = shift_frames(x, 1).reshape(count * frames, 128)
    sooner = shift_frames(x, -1).reshape(count * frames, 128)
    x = x.reshape(count * frames, 128)
    lanes = lax.broadcasted_iota(jnp.int32, x.shape, 1) >> 5
    acc = None
    for q in range(4):
        lhs = jnp.zeros_like(x)
        for part, shift, block in ((later, (0 - 32 * q) % 128, 0), (x, (32 - 32 * q) % 128, 1), (sooner, (64 - 32 * q) % 128, 2)):
            moved = pltpu.roll(part, shift, 1) if shift else part
            lhs = jnp.where(lanes == block, moved, lhs)
        lhs = lhs.T.astype(BF16)
        rhs = jnp.concatenate(
            [
                wide[2 - c : 2 - c + across, 2 - b + 2 * q : 4 - b + 2 * q].reshape(
                    count * frames, rank
                )
                for b in range(3)
                for c in range(3)
            ],
            axis=1,
        )
        y = jnp.dot(lhs, rhs, preferred_element_type=F32)
        acc = y if acc is None else acc + y
    for a in range(3):
        for j in range(2):
            for k in range(9):
                at = (27 * j + 9 * a + k) * 16
                flat[at : at + 16, :] = acc[
                    (2 * a + j) * 16 : (2 * a + j) * 16 + 16, k * rank : (k + 1) * rank
                ]
    for m in range(16):
        out[m] = flat[pl.ds(m, 54, stride=16), :].astype(BF16)


def end_kernel(
    step,
    at_d,
    up,
    p0,
    p1,
    p2,
    p3,
    terms,
    first,
    second,
    out,
    first_out,
    second_out,
    scales_out,
    flat,
    outflat,
):
    finish_kernel(at_d, up, p0, p1, p2, p3, out, flat, outflat)
    reduced = terms[0].astype(F32)
    for k in range(1, terms.shape[0]):
        reduced = reduced + terms[k].astype(F32)
    reduced = reduced * (1.0 / math.sqrt(TOKENS))
    new_first = 0.9 * first[...] + 0.1 * reduced
    new_second = 0.999 * second[...] + 0.001 * (reduced * reduced)
    count = jnp.full((1, 128), step[0], jnp.int32).astype(F32)
    first_bias = 1.0 - jnp.power(jnp.float32(0.9), count)
    second_bias = 1.0 - jnp.power(jnp.float32(0.999), count)
    adapted = new_first / first_bias / (jnp.sqrt(new_second / second_bias) + 1e-08)
    first_out[...] = new_first
    second_out[...] = new_second
    rest = jnp.zeros((128 - reduced.shape[0], 128), F32)

    def row_means(x):
        square = jnp.concatenate([x * x, rest], axis=0)
        return jnp.mean(square.T, axis=0, keepdims=True)

    scales = jnp.sqrt(row_means(adapted)) / jnp.sqrt(row_means(reduced) + 1e-06)
    scales_out[...] = scales[0, : reduced.shape[0]]


def finish_kernel(at_d, up, p0, p1, p2, p3, out, flat, outflat):
    cols, rows, frames, _ = up.shape
    for tile in range(4):
        flat[tile] = up[:, :, :, tile * 128 : tile * 128 + 128].astype(F32)
    for k, part in enumerate((p0, p1, p2, p3)):
        tile = lax.rem(at_d[0] + k, 4)
        total = flat[tile] + part[...].astype(F32)
        for w in range(cols):
            for h in range(rows):
                outflat[tile, pl.ds(h * cols + w, frames, stride=rows * cols), :] = total[w, h]
    for t in range(frames):
        for h in range(rows):
            base = (t * rows + h) * cols
            row = [outflat[tile, base : base + cols, :] for tile in range(4)]
            out[t, h] = jnp.concatenate(row, axis=1).astype(BF16)


def ring(axis, shift):
    n = lax.axis_size(axis)
    return [(i, (i + shift) % n) for i in range(n)]


def around(arrays, axis, sign=1):
    got = list(arrays)
    for k in (1, 3, 2):
        got[k] = lax.ppermute(arrays[k], axis, ring(axis, sign * k))
    return got


def step(
    inputs, pre_activation, upstream, weight, first_moment, second_moment, hash_seed, step_count
):
    frames, rows, cols, chans = inputs.shape[1:]
    rank = first_moment.shape[1]
    tokens = frames * rows * cols
    sx = ("sxx", "sxz")
    spread = pltpu.VMEM((chans // 128, tokens, 128), F32)
    g, proj, top, bot, up = _call(
        prepare,
        [
            (hash_seed.reshape(1), "scalar"),
            (pre_activation[0], "arg"),
            (upstream[0], "arg"),
        ],
        [
            ((cols, rows, frames, chans), BF16),
            ((cols, rows, frames, rank), BF16),
            ((cols, frames, chans + rank), BF16),
            ((cols, frames, chans + rank), BF16),
            ((cols, rows, frames, chans), BF16),
        ],
        [spread] * 2,
    )
    place = {a: lax.axis_index(a).astype(jnp.int32) for a in ("dp", "sy", "sxx", "sxz")}

    def places(*axes):
        return [(place[a].reshape(1), "smem") for a in axes]

    above = lax.ppermute(bot, "sy", ring("sy", 1))
    below = lax.ppermute(top, "sy", ring("sy", -1))
    (chunks,) = _call(
        pack_inputs, [(inputs[0], "arg")], [((16, cols, 2, frames, 128), BF16)], [spread]
    )
    along_z = ((cols, rows + 2 + 8, frames, 128), BF16)
    along_x = ((4, cols, rows + 4, frames, 128), BF16)
    g, *sends = _call(
        assemble,
        places("sy", "sxz")
        + [(a, "vmem") for a in (g, proj, chunks, above, below)],
        [((cols, rows + 2, frames, chans), BF16)] + [along_z] * 4,
    )
    got = around(sends, "sxz")
    sends = _call(
        across_x,
        places("sxx") + [(a, "vmem") for a in got],
        [along_x] * 4,
    )
    got = around(sends, "sxx")
    g_all = around([g] * 4, "dp")
    (terms,) = _call(
        moment_kernel,
        places("sxx", "sxz") + [(a, "vmem") for a in got],
        [((16, 54, rank), BF16)],
        [
            pltpu.VMEM((16 * cols + 2, rows + 2, frames, rank), BF16),
            pltpu.VMEM((16, cols, 2, frames, 128), BF16),
            pltpu.VMEM((54 * 16, rank), F32),
        ],
    )
    terms = lax.all_to_all(terms, ("dp", "sy"), 0, 0, tiled=True)

    own, left, right = _call(
        branch_kernel,
        [(x, "vmem") for x in g_all] + [(weight, "late")],
        [
            ((4, cols, rows, frames, 128), F32),
            ((4, rows, frames, 128), BF16),
            ((4, rows, frames, 128), BF16),
        ],
        [pltpu.VMEM((4, cols, rows + 2, frames, chans), BF16)],
    )
    from_right = lax.ppermute(left, sx, ring(sx, -1))
    from_left = lax.ppermute(right, sx, ring(sx, 1))
    mine = _call(
        merge_kernel,
        places("sxx", "sxz") + [(a, "vmem") for a in (own, from_left, from_right)],
        [((cols, rows, frames, 128), BF16)] * 4,
    )
    parts = around(mine, "dp", -1)
    input_grad, new_first, new_second, scales = _call(
        end_kernel,
        [(step_count.reshape(1), "scalar")]
        + places("dp")
        + [(a, "vmem") for a in (up, *parts, terms, first_moment, second_moment)],
        [
            ((frames, rows, cols, chans), BF16),
            (first_moment.shape, F32),
            (first_moment.shape, F32),
            ((first_moment.shape[0],), F32),
        ],
        [pltpu.VMEM((chans // 128, cols, rows, frames, 128), F32), spread],
    )
    return (input_grad[None], new_first, new_second, scales)


def solution(mesh):
    sizes = mesh.shape
    grid = Mesh(
        mesh.devices.reshape(sizes["dp"], sizes["sy"], 4, sizes["sx"] // 4),
        ("dp", "sy", "sxx", "sxz"),
    )
    sx = ("sxx", "sxz")
    whole = ("dp", "sy", "sxx", "sxz")
    volume = P("dp", None, "sy", sx, None)
    return jax.shard_map(
        step,
        mesh=grid,
        in_specs=(volume, volume, volume, P(None, "dp", None), P(whole), P(whole), P(), P()),
        out_specs=(volume, P(whole), P(whole), P(whole)),
        check_vma=False,
    )
```
